32 devices in a mesh: shard: 16 (over z, y, x), replica: 2 (over core).
Axes of the slice: x: 2, y: 2, z: 4, core: 2. Of those that a mesh axis runs over, the one named last changes fastest.
Arguments:
- latents: bfloat16 [8192, 1280], P(('shard', 'replica')), may hold values from -6 to 6
- noise: bfloat16 [8192, 1280], P(('shard', 'replica')), may hold values from -6 to 6
- timesteps: int32 [16], replicated, may hold values from 0 to 999
- master_weight: float32 [1280, 1280], P('shard'), may hold values from -0.15625 to 0.15625
- norm_gain: float32 [1280], P('shard'), may hold values from 0.5 to 1.5
- weight_moment: float32 [1280, 1280], P('shard'), may hold values from -4 to 4
- weight_second: float32 [1280, 1280], P('shard'), may hold values from 0.1 to 2
- gain_moment: float32 [1280], P('shard'), may hold values from -4 to 4
- gain_second: float32 [1280], P('shard'), may hold values from 0.1 to 2
Outputs:
- new_weight: float32 [1280, 1280], P('shard')
- new_weight_moment: float32 [1280, 1280], P('shard')
- new_weight_second: float32 [1280, 1280], P('shard')
- new_gain: float32 [1280], P('shard')
- new_gain_moment: float32 [1280], P('shard')
- new_gain_second: float32 [1280], P('shard')
The draws below stay inside these ranges and needn't reach their ends.
All inputs are finite; a program needn't handle non-finite values.
Results may differ from the reference program's by a relative error of at most 0.0043.
Values may be sent and summed in bfloat16 or wider, within the bound.
No kernel may reach another device: no remote copies, remote signals or barrier semaphores. Data moves between devices by JAX's collectives and lax.ppermute only.
A program may use at most 64 MiB of HBM per device.

```python
import math
import jax
import jax.numpy as jnp
from jax import lax

C = 1280
VOX = 512
ROWS = 8192
SAMPLES = 16


def touch_ends(drawn, stream_key, smallest, high):
    longest = drawn.shape.index(max(drawn.shape))
    spots = []
    for shift in (0, 1):
        where = [jax.random.randint(jax.random.fold_in(stream_key, axis), (), 0, length) for axis, length in enumerate(drawn.shape)]
        where[longest] = (where[longest] + shift) % drawn.shape[longest]
        spots.append(tuple(where))
    return drawn.at[spots[0]].set(smallest).at[spots[1]].set(high)


def shard_levels(rng, extent, shards, low, top_value):
    def one(position, shards_of):
        heights = jax.random.uniform(jax.random.fold_in(jax.random.fold_in(rng, 6), position), (shards_of,), jnp.float32, low / len(shards), top_value / len(shards))
        return jnp.repeat(jnp.exp(heights), extent[position] // shards_of).reshape((-1,) + (1,) * (len(extent) - position - 1))

    level = one(*shards[0])
    for cut in shards[1:]:
        level = level * one(*cut)
    return level


def gaussian(stream_key, extent, scale, most, shards=(), held_as=jnp.bfloat16):
    entries = scale * jax.random.normal(stream_key, extent, jnp.float32)
    if shards:
        entries = entries * shard_levels(stream_key, extent, shards, -0.22, 0.18)
    return jnp.clip(entries, -most, most).astype(held_as)


def setup_inputs(seed: int = 0) -> dict:
    splits = jax.random.split(jax.random.key(seed), 10)
    latents = gaussian(splits[0], (ROWS, C), 1.0, 6.0, ((0, 32),))
    noise = gaussian(splits[1], (ROWS, C), 1.0, 6.0, ((0, 32),))
    timesteps = touch_ends(jax.random.randint(splits[2], (SAMPLES,), 0, 1000), jax.random.fold_in(splits[2], 1), 0, 999).astype(jnp.int32)
    master_weight = gaussian(splits[3], (C, C), C ** -0.5, 0.15625, ((0, 16),), jnp.float32)
    norm_gain = jnp.clip(1.0 + 0.1 * jax.random.normal(splits[4], (C,), jnp.float32), 0.5, 1.5)
    weight_moment = gaussian(splits[5], (C, C), 0.5, 4.0, ((0, 16),), jnp.float32)
    weight_second = jnp.clip(jnp.exp(math.log(2.0) - 2.9957323 * jax.random.uniform(splits[6], (C, C), jnp.float32) ** shard_levels(splits[6], (C, C), ((0, 16),), -0.2, 0.2)), 0.1, 2.0)
    gain_moment = gaussian(splits[7], (C,), 0.5, 4.0, ((0, 16),), jnp.float32)
    gain_second = jnp.clip(jnp.exp(math.log(2.0) - 2.9957323 * jax.random.uniform(splits[8], (C,), jnp.float32) ** shard_levels(splits[8], (C,), ((0, 16),), -0.2, 0.2)), 0.1, 2.0)
    return dict(latents=latents, noise=noise, timesteps=timesteps, master_weight=master_weight, norm_gain=norm_gain, weight_moment=weight_moment, weight_second=weight_second, gain_moment=gain_moment, gain_second=gain_second)


bias_first = 0.9999734386011124
bias_second = 0.095207852886291

def adam_step(param, grad, moment, second):
    new_moment = 0.9 * moment + 0.1 * grad
    new_second = 0.999 * second + 0.001 * grad * grad
    update = new_moment / bias_first / (jnp.sqrt(new_second / bias_second) + 1e-08)
    return (param - 0.05 * update, new_moment, new_second)

def reference(latents, noise, timesteps, master_weight, norm_gain, weight_moment, weight_second, gain_moment, gain_second):
    total_rows, width = latents.shape
    sample_of = jnp.arange(total_rows, dtype=jnp.int32) // VOX
    step_time = timesteps[sample_of].astype(jnp.float32)
    level = jnp.cos((step_time / 1000.0 + 0.008) / 1.008 * (math.pi / 2)) ** 2
    noisy = jnp.sqrt(level)[:, None] * latents.astype(jnp.float32) + jnp.sqrt(1.0 - level)[:, None] * noise.astype(jnp.float32)
    half = width // 2
    freqs = jnp.exp(-(2.0 * jnp.arange(half, dtype=jnp.float32) / width) * math.log(10000.0))
    angles = step_time[:, None] * freqs[None, :]
    embed = jnp.concatenate([jnp.sin(angles), jnp.cos(angles)], axis=1)
    mean = lax.optimization_barrier(jnp.mean(noisy, axis=1, keepdims=True))
    var = lax.optimization_barrier(jnp.mean((noisy - mean) ** 2, axis=1, keepdims=True))
    normed = (noisy - mean) / jnp.sqrt(var + 1e-05)
    hidden = normed * norm_gain[None, :] + embed
    act = jax.nn.silu(hidden).astype(jnp.bfloat16)
    mixing = master_weight.astype(jnp.bfloat16)
    predicted = noisy + jnp.dot(act, mixing, preferred_element_type=jnp.float32)
    scale = 1.0 / math.sqrt(total_rows)
    grad_out = ((predicted - noise.astype(jnp.float32)) * scale).astype(jnp.bfloat16)
    weight_grad = jnp.dot(act.T, grad_out, preferred_element_type=jnp.float32)
    grad_act = jnp.dot(grad_out, mixing.T, preferred_element_type=jnp.float32)
    sig = jax.nn.sigmoid(hidden)
    grad_hidden = grad_act * (sig * (1.0 + hidden * (1.0 - sig)))
    gain_grad = lax.optimization_barrier(jnp.sum(grad_hidden * normed, axis=0))
    new_weight, new_wm, new_ws = adam_step(master_weight, weight_grad, weight_moment, weight_second)
    new_gain, new_gm, new_gs = adam_step(norm_gain, gain_grad, gain_moment, gain_second)
    return (new_weight, new_wm, new_ws, new_gain, new_gm, new_gs)
```

```python
import functools
import math

import jax
import jax.numpy as jnp
from jax import lax
from jax.experimental import pallas as pl
from jax.experimental.pallas import tpu as pltpu
from jax.sharding import PartitionSpec as P

VOX = 512
AXES = ("shard", "replica")
BF = jnp.bfloat16
F32 = jnp.float32

bias_first = 0.9999734386011124
bias_second = 0.095207852886291


def adam_step(param, grad, moment, second):
    new_moment = 0.9 * moment + 0.1 * grad
    new_second = 0.999 * second + 0.001 * grad * grad
    update = new_moment / bias_first / (jnp.sqrt(new_second / bias_second) + 1e-08)
    return (param - 0.05 * update, new_moment, new_second)


def frequencies(width):
    half = width // 2
    return jnp.exp(-(2.0 * jnp.arange(half, dtype=F32) / width) * math.log(10000.0))


def noise_level(step_time):
    return jnp.cos((step_time / 1000.0 + 0.008) / 1.008 * (math.pi / 2)) ** 2


def general_body(
    latents, noise, timesteps, master_weight, norm_gain, weight_moment, weight_second, gain_moment, gain_second
):
    rows, width = latents.shape
    shard_count = lax.axis_size("shard")
    replica_count = lax.axis_size("replica")
    total_rows = rows * shard_count * replica_count
    block_index = lax.axis_index("shard") * replica_count + lax.axis_index("replica")
    row_ids = block_index * rows + jnp.arange(rows, dtype=jnp.int32)
    step_time = timesteps[row_ids // VOX].astype(F32)
    level = noise_level(step_time)
    noisy = (
        jnp.sqrt(level)[:, None] * latents.astype(F32)
        + jnp.sqrt(1.0 - level)[:, None] * noise.astype(F32)
    )
    angles = step_time[:, None] * frequencies(width)[None, :]
    embed = jnp.concatenate([jnp.sin(angles), jnp.cos(angles)], axis=1)
    mean = jnp.mean(noisy, axis=1, keepdims=True)
    var = jnp.mean((noisy - mean) ** 2, axis=1, keepdims=True)
    normed = (noisy - mean) / jnp.sqrt(var + 1e-05)
    full_gain = lax.all_gather(norm_gain, "shard", axis=0, tiled=True)
    hidden = normed * full_gain[None, :] + embed
    act = jax.nn.silu(hidden).astype(BF)
    mixing = lax.all_gather(master_weight.astype(BF), "shard", axis=0, tiled=True)
    scale = 1.0 / math.sqrt(total_rows)
    predicted = noisy + jnp.dot(act, mixing, preferred_element_type=F32)
    grad_out = ((predicted - noise.astype(F32)) * scale).astype(BF)
    grad_act = lax.dot_general(
        grad_out, mixing, (((1,), (1,)), ((), ())), preferred_element_type=F32
    )
    weight_share = lax.psum_scatter(
        lax.dot_general(act, grad_out, (((0,), (0,)), ((), ())), preferred_element_type=F32),
        "shard",
        scatter_dimension=0,
        tiled=True,
    )
    sig = jax.nn.sigmoid(hidden)
    grad_hidden = grad_act * (sig * (1.0 + hidden * (1.0 - sig)))
    gain_local = jnp.sum(grad_hidden * normed, axis=0)
    gain_share = lax.psum_scatter(gain_local, "shard", scatter_dimension=0, tiled=True)
    weight_grad, gain_grad = lax.psum((weight_share, gain_share), "replica")
    return (
        *adam_step(master_weight, weight_grad, weight_moment, weight_second),
        *adam_step(norm_gain, gain_grad, gain_moment, gain_second),
    )


VMEM = pl.BlockSpec(memory_space=pltpu.VMEM)
SMEM = pl.BlockSpec(memory_space=pltpu.SMEM)


def act_kernel(half, pos_ref, coef_ref, gain_ref, embed_ref, l0, n0, l1, n1, act_ref, slope_ref, diff_ref):
    width = act_ref.shape[1]
    col = pl.ds(pl.multiple_of(pos_ref[1] * half, 128), half)
    a, b = coef_ref[0], coef_ref[1]
    gain = gain_ref[...]
    embed = embed_ref[...]
    tile = 16
    for part, (l_ref, n_ref) in enumerate(((l0, n0), (l1, n1))):
        rows = l_ref.shape[0]

        def step(i, carry, l_ref=l_ref, n_ref=n_ref, base=part * rows):
            at = pl.ds(pl.multiple_of(i * tile, tile), tile)
            to = pl.ds(pl.multiple_of(base + i * tile, tile), tile)
            noisy = a * l_ref[at, :].astype(F32) + b * n_ref[at, :].astype(F32)
            mean = jnp.sum(noisy, axis=1, keepdims=True) * (1.0 / width)
            cent = noisy - mean
            var = jnp.sum(cent * cent, axis=1, keepdims=True) * (1.0 / width)
            normed = cent * (1.0 / jnp.sqrt(var + 1e-05))
            hidden = normed * gain + embed
            sig = 1.0 / (1.0 + jnp.exp(-hidden))
            act_ref[to, :] = (hidden * sig).astype(BF)
            slope_ref[to, :] = sig * (1.0 + hidden * (1.0 - sig)) * normed
            nh = n_ref[at, col].astype(F32)
            diff_ref[to, :] = (a * l_ref[at, col].astype(F32) + b * nh) - nh
            return carry

        lax.fori_loop(0, rows // tile, step, 0)


def mix_kernel(
    scale, unit, pos_ref, act_ref, diff_ref, wa, wa1, wa2, wb, wb1, wb2,
    gout_ref, w_ref, send_a, send_b, keep_a, keep_b, wg_ref,
):
    me = pos_ref[0]

    def place(kz, kp):
        return pl.ds(pl.multiple_of((me ^ (kz * 4 + kp)) * unit, 16), unit)

    def rows(i):
        return pl.ds(i * unit, unit)

    for k in range(2):
        w_ref[place(k, 0), :] = wa[rows(k), :]
        w_ref[place(k, 1), :] = wa1[rows(k), :]
        w_ref[place(k, 2), :] = wa2[rows(k), :]
        w_ref[place(k, 3), :] = wa2[rows(2 + k), :]
        w_ref[place(2 + k, 0), :] = wb[rows(k), :]
        w_ref[place(2 + k, 2), :] = wb1[rows(k), :]
        w_ref[place(2 + k, 1), :] = wb2[rows(k), :]
        w_ref[place(2 + k, 3), :] = wb2[rows(2 + k), :]
    product = jnp.dot(act_ref[...], w_ref[...], preferred_element_type=F32)
    gout_ref[...] = ((diff_ref[...] + product) * scale).astype(BF)
    wg_ref[...] = lax.dot_general(
        act_ref[...], gout_ref[...], (((0,), (0,)), ((), ())), preferred_element_type=F32
    )
    for k in range(2):
        send_a[rows(k), :] = wg_ref[place(k, 1), :].astype(BF)
        send_a[rows(2 + k), :] = wg_ref[place(k, 3), :].astype(BF)
        keep_a[rows(k), :] = wg_ref[place(k, 0), :]
        keep_a[rows(2 + k), :] = wg_ref[place(k, 2), :]
        send_b[rows(k), :] = wg_ref[place(2 + k, 2), :].astype(BF)
        send_b[rows(2 + k), :] = wg_ref[place(2 + k, 3), :].astype(BF)
        keep_b[rows(k), :] = wg_ref[place(2 + k, 0), :]
        keep_b[rows(2 + k), :] = wg_ref[place(2 + k, 1), :]


def gain_kernel(gout_ref, w_ref, slope_ref, out_ref):
    grad_act = lax.dot_general(
        gout_ref[...], w_ref[...], (((1,), (1,)), ((), ())), preferred_element_type=F32
    )
    out_ref[...] = jnp.sum(grad_act * slope_ref[...], axis=0, keepdims=True)


def paired_body(
    latents, noise, timesteps, master_weight, norm_gain, weight_moment, weight_second, gain_moment, gain_second
):
    rows, width = latents.shape
    unit = master_weight.shape[0]
    shards, cores = lax.axis_size("shard"), lax.axis_size("replica")
    total_rows = rows * shards * cores
    half = width // 2
    me, core = lax.axis_index("shard"), lax.axis_index("replica")
    pos = jnp.stack([me, core]).astype(jnp.int32)

    def to(x, k):
        pairs = [(i * cores + c, (i ^ k) * cores + c) for i in range(shards) for c in range(cores)]
        return lax.ppermute(x, AXES, pairs)

    def across(x):
        pairs = [(i * cores + c, i * cores + 1 - c) for i in range(shards) for c in range(cores)]
        return lax.ppermute(x, AXES, pairs)

    def call(kernel, outs, specs, scratch=(), flops=0, byts=0):
        return pl.pallas_call(
            kernel,
            out_shape=outs,
            in_specs=specs,
            out_specs=jax.tree.map(lambda _: VMEM, outs),
            scratch_shapes=list(scratch),
            compiler_params=pltpu.CompilerParams(vmem_limit_bytes=40 << 20),
            cost_estimate=pl.CostEstimate(flops=flops, bytes_accessed=byts, transcendentals=0),
        )

    arr = jax.ShapeDtypeStruct

    own = lax.dynamic_slice(master_weight, (0, core * half), (unit, half)).astype(BF)
    z1, z2, z3 = to(own, 4), to(own, 8), to(own, 12)
    wa = jnp.concatenate([own, z1], axis=0)
    wa1 = to(wa, 1)
    wb = jnp.concatenate([z2, z3], axis=0)
    wb1 = to(wb, 2)
    wa2 = to(jnp.concatenate([wa, wa1], axis=0), 2)
    wb2 = to(jnp.concatenate([wb, wb1], axis=0), 1)

    gain = lax.dynamic_update_slice(
        jnp.zeros((1, width), F32), norm_gain.reshape(1, unit), (0, me * unit)
    )
    gain = gain + to(gain, 4) + to(gain, 8) + to(gain, 12)
    gain = gain + to(gain, 1)
    gain = gain + to(gain, 2)

    other_latents, other_noise = across(latents), across(noise)
    step_time = lax.dynamic_slice(timesteps, (me * cores * rows // VOX,), (1,)).astype(F32)
    level = noise_level(step_time)
    coef = jnp.concatenate([jnp.sqrt(level), jnp.sqrt(1.0 - level)])
    angles = step_time[:, None] * frequencies(width)[None, :]
    embed = jnp.concatenate([jnp.sin(angles), jnp.cos(angles)], axis=1)
    both = rows * cores
    act, slope, diff = call(
        functools.partial(act_kernel, half),
        (arr((both, width), BF), arr((both, width), F32), arr((both, half), F32)),
        [SMEM, SMEM] + [VMEM] * 6,
        flops=30 * both * width,
        byts=8 * both * width,
    )(pos, coef, gain, embed, latents, noise, other_latents, other_noise)

    gout, mixing, send_a, send_b, keep_a, keep_b = call(
        functools.partial(mix_kernel, 1.0 / math.sqrt(total_rows), unit),
        (
            arr((both, half), BF),
            arr((width, half), BF),
            arr((4 * unit, half), BF),
            arr((4 * unit, half), BF),
            arr((4 * unit, half), F32),
            arr((4 * unit, half), F32),
        ),
        [SMEM] + [VMEM] * 8,
        [pltpu.VMEM((width, half), F32)],
        flops=4 * both * width * half,
        byts=6 * both * width,
    )(pos, act, diff, wa, wa1, wa2, wb, wb1, wb2)

    got_a, got_b = to(send_a, 1), to(send_b, 2)
    part = call(
        gain_kernel,
        arr((1, width), F32),
        [VMEM] * 3,
        flops=2 * both * width * half,
        byts=6 * both * width,
    )(gout, mixing, slope)

    two, one = 2 * unit, unit
    sum_a = keep_a + got_a.astype(F32)
    sum_b = keep_b + got_b.astype(F32)
    got_a2 = to(sum_a[two:].astype(BF), 2)
    got_b2 = to(sum_b[two:].astype(BF), 1)
    sum_a = sum_a[:two] + got_a2.astype(F32)
    sum_b = sum_b[:two] + got_b2.astype(F32)
    h1 = to(sum_a[one:].astype(BF), 4)
    h2 = to(sum_b[:one].astype(BF), 8)
    h3 = to(sum_b[one:].astype(BF), 12)
    mine = sum_a[:one] + h1.astype(F32) + h2.astype(F32) + h3.astype(F32)

    for k in (1, 2, 4, 8):
        part = part + to(part, k)
    part = part + across(part)
    gain_grad = lax.dynamic_slice(part, (0, me * unit), (1, unit)).reshape(unit)

    theirs = across(mine)
    weight_grad = jnp.where(
        core == 0,
        jnp.concatenate([mine, theirs], axis=1),
        jnp.concatenate([theirs, mine], axis=1),
    )
    return (
        *adam_step(master_weight, weight_grad, weight_moment, weight_second),
        *adam_step(norm_gain, gain_grad, gain_moment, gain_second),
    )


def body(latents, *rest):
    rows, width = latents.shape
    unit = rest[2].shape[0]
    paired = (
        lax.axis_size("shard") == 16
        and lax.axis_size("replica") == 2
        and unit % 16 == 0
        and width % 256 == 0
        and rows % 16 == 0
        and VOX % (2 * rows) == 0
    )
    return (paired_body if paired else general_body)(latents, *rest)


def solution(mesh):
    rows = P(AXES, None)
    block = P("shard", None)
    line = P("shard")
    return jax.shard_map(
        body,
        mesh=mesh,
        in_specs=(rows, rows, P(), block, line, block, block, line, line),
        out_specs=(block, block, block, line, line, line),
        check_vma=False,
    )
```

```python
import functools
import math

import jax
import jax.numpy as jnp
from jax import lax
from jax.experimental import pallas as pl
from jax.experimental.pallas import tpu as pltpu
from jax.sharding import PartitionSpec as P

VOX = 512
AXES = ("shard", "replica")
BF = jnp.bfloat16
F32 = jnp.float32

bias_first = 0.9999734386011124
bias_second = 0.095207852886291


def adam_step(param, grad, moment, second):
    new_moment = 0.9 * moment + 0.1 * grad
    new_second = 0.999 * second + 0.001 * grad * grad
    update = new_moment / bias_first / (jnp.sqrt(new_second / bias_second) + 1e-08)
    return (param - 0.05 * update, new_moment, new_second)


def frequencies(width):
    half = width // 2
    return jnp.exp(-(2.0 * jnp.arange(half, dtype=F32) / width) * math.log(10000.0))


def noise_level(step_time):
    return jnp.cos((step_time / 1000.0 + 0.008) / 1.008 * (math.pi / 2)) ** 2


def general_body(
    latents, noise, timesteps, master_weight, norm_gain, weight_moment, weight_second, gain_moment, gain_second
):
    rows, width = latents.shape
    shard_count = lax.axis_size("shard")
    replica_count = lax.axis_size("replica")
    total_rows = rows * shard_count * replica_count
    block_index = lax.axis_index("shard") * replica_count + lax.axis_index("replica")
    row_ids = block_index * rows + jnp.arange(rows, dtype=jnp.int32)
    step_time = timesteps[row_ids // VOX].astype(F32)
    level = noise_level(step_time)
    noisy = (
        jnp.sqrt(level)[:, None] * latents.astype(F32)
        + jnp.sqrt(1.0 - level)[:, None] * noise.astype(F32)
    )
    angles = step_time[:, None] * frequencies(width)[None, :]
    embed = jnp.concatenate([jnp.sin(angles), jnp.cos(angles)], axis=1)
    mean = jnp.mean(noisy, axis=1, keepdims=True)
    var = jnp.mean((noisy - mean) ** 2, axis=1, keepdims=True)
    normed = (noisy - mean) / jnp.sqrt(var + 1e-05)
    full_gain = lax.all_gather(norm_gain, "shard", axis=0, tiled=True)
    hidden = normed * full_gain[None, :] + embed
    act = jax.nn.silu(hidden).astype(BF)
    mixing = lax.all_gather(master_weight.astype(BF), "shard", axis=0, tiled=True)
    scale = 1.0 / math.sqrt(total_rows)
    predicted = noisy + jnp.dot(act, mixing, preferred_element_type=F32)
    grad_out = ((predicted - noise.astype(F32)) * scale).astype(BF)
    grad_act = lax.dot_general(
        grad_out, mixing, (((1,), (1,)), ((), ())), preferred_element_type=F32
    )
    weight_share = lax.psum_scatter(
        lax.dot_general(act, grad_out, (((0,), (0,)), ((), ())), preferred_element_type=F32),
        "shard",
        scatter_dimension=0,
        tiled=True,
    )
    sig = jax.nn.sigmoid(hidden)
    grad_hidden = grad_act * (sig * (1.0 + hidden * (1.0 - sig)))
    gain_local = jnp.sum(grad_hidden * normed, axis=0)
    gain_share = lax.psum_scatter(gain_local, "shard", scatter_dimension=0, tiled=True)
    weight_grad, gain_grad = lax.psum((weight_share, gain_share), "replica")
    return (
        *adam_step(master_weight, weight_grad, weight_moment, weight_second),
        *adam_step(norm_gain, gain_grad, gain_moment, gain_second),
    )


VMEM = pl.BlockSpec(memory_space=pltpu.VMEM)
ANY = pl.BlockSpec(memory_space=pl.ANY)
SMEM = pl.BlockSpec(memory_space=pltpu.SMEM)


def split(x, parts):
    out = []
    for _ in range(parts):
        top = x.astype(BF).astype(F32)
        out.append(top)
        x = x - top
    return out


def stack_rows(pieces, shape):
    row = lax.broadcasted_iota(jnp.int32, shape, 0)
    tile = jnp.zeros(shape, F32)
    for i, piece in enumerate(pieces):
        tile = jnp.where(row == i, jnp.broadcast_to(piece, shape), tile)
    return tile


def pack_kernel(w_ref, gain_ref, out_ref, part_ref, sem):
    unit, half = part_ref.shape
    col = pl.ds(pl.multiple_of(lax.axis_index("replica") * half, 128), half)
    copy = pltpu.make_async_copy(w_ref.at[:, col], part_ref, sem)
    copy.start()
    out_ref[unit:, :] = jnp.zeros((16, half), BF)
    gain = stack_rows(split(gain_ref[...], 3), (16, unit))
    out_ref[unit:, :unit] = gain.astype(BF)
    copy.wait()
    out_ref[:unit, :] = part_ref[...].astype(BF)


def norm_kernel(coef_ref, l_ref, n_ref, normed_ref, diff_ref):
    rows, width = normed_ref.shape
    half = width // 2
    col = pl.ds(pl.multiple_of(lax.axis_index("replica") * half, 128), half)
    a, b = coef_ref[0], coef_ref[1]
    tile = 32

    def step(i, carry):
        at = pl.ds(pl.multiple_of(i * tile, tile), tile)
        noisy = a * l_ref[at, :].astype(F32) + b * n_ref[at, :].astype(F32)
        mean = jnp.sum(noisy, axis=1, keepdims=True) * (1.0 / width)
        cent = noisy - mean
        var = jnp.sum(cent * cent, axis=1, keepdims=True) * (1.0 / width)
        normed_ref[at, :] = cent * (1.0 / jnp.sqrt(var + 1e-05))
        nh = n_ref[at, col].astype(F32)
        diff_ref[at, :] = (a * l_ref[at, col].astype(F32) + b * nh) - nh
        return carry

    lax.fori_loop(0, rows // tile, step, 0)


def join_kernel(unit, own, z1, after, wa):
    wa[:unit, :] = own[:unit, :]
    wa[unit:, :] = z1[:unit, :]


def join_gain_kernel(unit, own, z1, z2, z3, after, wb, tile):
    for i, z in enumerate((z2, z3)):
        wb[i * unit : (i + 1) * unit, :] = z[:unit, :]
    tile[...] = jnp.zeros_like(tile)
    for i, z in enumerate((own, z1, z2, z3)):
        tile[:, 128 * i : 128 * i + 128] = z[unit:, :128]
    wb[2 * unit :, :] = tile[...]


def pair_kernel(first, second, out):
    n = out.shape[0] // 2
    out[:n, :] = first[:n, :]
    out[n:, :] = second[:n, :]


def act_kernel(unit, embed_ref, t0, t1, t2, t3, normed0, normed1, act_ref, slope_ref, slots, gain_ref):
    me = lax.axis_index("shard")
    both, width = act_ref.shape
    for kp, t in enumerate((t0, t1, t2, t3)):
        x = t[...].astype(F32)
        line = x[0:1, :] + x[1:2, :] + x[2:3, :]
        for kz in range(4):
            slots[4 * kz + kp : 4 * kz + kp + 1, :] = line[:, 128 * kz : 128 * kz + 128]
    for i in range(16):
        gain_ref[:, i * unit : (i + 1) * unit] = slots[pl.ds(me ^ i, 1), :unit]
    gain = gain_ref[...]
    embed = embed_ref[...]
    tile = 32

    for part, normed_ref in enumerate((normed0, normed1)):

        def step(i, carry, normed_ref=normed_ref, base=part * normed0.shape[0]):
            at = pl.ds(pl.multiple_of(i * tile, tile), tile)
            to = pl.ds(pl.multiple_of(base + i * tile, tile), tile)
            normed = normed_ref[at, :]
            hidden = normed * gain + embed
            sig = 0.5 * jnp.tanh(0.5 * hidden) + 0.5
            act = hidden * sig
            act_ref[to, :] = act.astype(BF)
            slope_ref[to, :] = (sig + act * (1.0 - sig)) * normed
            return carry

        lax.fori_loop(0, normed_ref.shape[0] // tile, step, 0)


def mix_kernel(
    scale, unit, act_ref, slope_ref, diff0, diff1, wa, wa1, wa2, wb, wb1, wb2,
    send_a, send_b, keep_a, keep_b, keep_g, w_ref, wg_ref, gout_ref, slots,
):
    me = lax.axis_index("shard")

    def place(kz, kp):
        return pl.ds(pl.multiple_of((me ^ (kz * 4 + kp)) * unit, 16), unit)

    def rows(i):
        return pl.ds(i * unit, unit)

    for k in range(2):
        w_ref[place(k, 0), :] = wa[rows(k), :]
        w_ref[place(k, 1), :] = wa1[rows(k), :]
        w_ref[place(k, 2), :] = wa2[rows(k), :]
        w_ref[place(k, 3), :] = wa2[rows(2 + k), :]
        w_ref[place(2 + k, 0), :] = wb[rows(k), :]
        w_ref[place(2 + k, 2), :] = wb1[rows(k), :]
        w_ref[place(2 + k, 1), :] = wb2[rows(k), :]
        w_ref[place(2 + k, 3), :] = wb2[rows(2 + k), :]
    product = jnp.dot(act_ref[...], w_ref[...], preferred_element_type=F32)
    own_rows = diff0.shape[0]
    gout_ref[:own_rows, :] = ((diff0[...] + product[:own_rows]) * scale).astype(BF)
    gout_ref[own_rows:, :] = ((diff1[...] + product[own_rows:]) * scale).astype(BF)
    grad_act = lax.dot_general(
        gout_ref[...], w_ref[...], (((1,), (1,)), ((), ())), preferred_element_type=F32
    )
    part = jnp.sum(grad_act * slope_ref[...], axis=0, keepdims=True)
    wg_ref[...] = lax.dot_general(
        act_ref[...], gout_ref[...], (((0,), (0,)), ((), ())), preferred_element_type=F32
    )
    half = wg_ref.shape[1]
    slots[...] = jnp.zeros_like(slots)
    for i in range(16):
        slots[pl.ds(me ^ i, 1), :unit] = part[:, i * unit : (i + 1) * unit]
    lines = [
        jnp.concatenate([slots[4 * kz + kp : 4 * kz + kp + 1, :] for kz in range(4)], axis=1)
        for kp in range(4)
    ]
    keep_g[...] = jnp.zeros_like(keep_g)
    keep_g[0:1, :512] = lines[0]
    keep_g[1:2, :512] = lines[2]
    for k in range(2):
        send_a[rows(k), :] = wg_ref[place(k, 1), :].astype(BF)
        send_a[rows(2 + k), :] = wg_ref[place(k, 3), :].astype(BF)
        keep_a[rows(k), :] = wg_ref[place(k, 0), :]
        keep_a[rows(2 + k), :] = wg_ref[place(k, 2), :]
        send_b[rows(k), :] = wg_ref[place(2 + k, 2), :].astype(BF)
        send_b[rows(2 + k), :] = wg_ref[place(2 + k, 3), :].astype(BF)
        keep_b[rows(k), :] = wg_ref[place(2 + k, 0), :]
        keep_b[rows(2 + k), :] = wg_ref[place(2 + k, 1), :]
    send_a[4 * unit :, :] = jnp.zeros((16, half), BF)
    send_a[4 * unit :, :512] = stack_rows(split(lines[1], 2) + split(lines[3], 2), (16, 512)).astype(BF)


def fold_a_kernel(unit, keep_a, keep_g, got, send, own, own_g):
    two = 2 * unit
    send[:two, :] = (keep_a[two:, :] + got[two : 2 * two, :].astype(F32)).astype(BF)
    extra = got[2 * two :, :].astype(F32)
    own_g[...] = jnp.zeros_like(own_g)
    own_g[0:1, :] = keep_g[0:1, :] + (extra[0:1, :] + extra[1:2, :])
    line = keep_g[1:2, :] + (extra[2:3, :] + extra[3:4, :])
    send[two:, :] = stack_rows(split(line, 2), (16, line.shape[1])).astype(BF)
    own[...] = keep_a[:two, :] + got[:two, :].astype(F32)


def fold_b_kernel(unit, keep_b, got, send, own):
    two = 2 * unit
    send[...] = (keep_b[two:, :] + got[two:, :].astype(F32)).astype(BF)
    own[...] = keep_b[:two, :] + got[:two, :].astype(F32)


def turn_a_kernel(unit, own, own_g, got, send1, mine, line_ref):
    two = 2 * unit
    half = own.shape[1]
    extra = got[two:, :].astype(F32)
    line = own_g[0:1, :] + (extra[0:1, :] + extra[1:2, :])
    send1[:unit, :] = (own[unit:, :] + got[unit:two, :].astype(F32)).astype(BF)
    send1[unit:, :] = jnp.zeros((16, half), BF)
    send1[unit:, :128] = stack_rows(split(line[:, 128:256], 2), (16, 128)).astype(BF)
    mine[...] = own[:unit, :] + got[:unit, :].astype(F32)
    line_ref[...] = jnp.zeros_like(line_ref)
    line_ref[0:1, :] = line


def turn_b_kernel(unit, own, got, line_ref, send2, send3):
    half = own.shape[1]
    total = own[...] + got[...].astype(F32)
    for k, send in ((2, send2), (3, send3)):
        send[:unit, :] = total[(k - 2) * unit : (k - 1) * unit, :].astype(BF)
        send[unit:, :] = jnp.zeros((16, half), BF)
        piece = line_ref[0:1, 128 * k : 128 * k + 128]
        send[unit:, :128] = stack_rows(split(piece, 2), (16, 128)).astype(BF)


def last_kernel(unit, mine, line_ref, h1, h2, h3, out_ref):
    total = mine[...]
    line = line_ref[0:1, :128]
    for h in (h1, h2, h3):
        total = total + h[:unit, :].astype(F32)
        extra = h[unit:, :128].astype(F32)
        line = line + (extra[0:1, :] + extra[1:2, :])
    out_ref[:unit, :] = total
    out_ref[unit:, :] = jnp.zeros((8, total.shape[1]), F32)
    out_ref[unit : unit + 1, :128] = line


def adam_kernel(unit, half, mine, theirs, w, wm, ws, g, gm, gs, nw, nwm, nws, ng, ngm, ngs):
    core = lax.axis_index("replica")
    for ref, side in ((mine, core), (theirs, 1 - core)):
        col = pl.ds(pl.multiple_of(side * half, 128), half)
        nw[:, col], nwm[:, col], nws[:, col] = adam_step(
            w[:, col], ref[:unit, :], wm[:, col], ws[:, col]
        )
    line = mine[unit : unit + 1, :unit] + theirs[unit : unit + 1, :unit]
    ng[...], ngm[...], ngs[...] = adam_step(g[...], line, gm[...], gs[...])


def paired_body(
    latents, noise, timesteps, master_weight, norm_gain, weight_moment, weight_second, gain_moment, gain_second
):
    rows, width = latents.shape
    unit = master_weight.shape[0]
    shards, cores = lax.axis_size("shard"), lax.axis_size("replica")
    total_rows = rows * shards * cores
    half = width // 2
    both = rows * cores
    me = lax.axis_index("shard")

    def to(x, k):
        pairs = [(i * cores + c, (i ^ k) * cores + c) for i in range(shards) for c in range(cores)]
        return lax.ppermute(x, AXES, pairs)

    def across(x):
        pairs = [(i * cores + c, i * cores + 1 - c) for i in range(shards) for c in range(cores)]
        return lax.ppermute(x, AXES, pairs)

    def call(kernel, outs, specs, scratch=(), flops=0, byts=0):
        return pl.pallas_call(
            kernel,
            out_shape=outs,
            in_specs=specs,
            out_specs=jax.tree.map(lambda _: VMEM, outs),
            scratch_shapes=list(scratch),
            compiler_params=pltpu.CompilerParams(vmem_limit_bytes=40 << 20),
            cost_estimate=pl.CostEstimate(flops=flops, bytes_accessed=byts, transcendentals=0),
        )

    arr = jax.ShapeDtypeStruct
    two, four = 2 * unit, 4 * unit

    own = call(
        pack_kernel,
        arr((unit + 16, half), BF),
        [ANY, VMEM],
        [pltpu.VMEM((unit, half), F32), pltpu.SemaphoreType.DMA],
        byts=6 * unit * half,
    )(master_weight, norm_gain.reshape(1, unit))
    z1, z2, z3 = to(own, 4), to(own, 8), to(own, 12)

    other_latents, other_noise = across(latents), across(noise)
    step_time = lax.dynamic_slice(timesteps, (me * cores * rows // VOX,), (1,)).astype(F32)
    level = noise_level(step_time)
    coef = jnp.concatenate([jnp.sqrt(level), jnp.sqrt(1.0 - level)])
    angles = step_time[:, None] * frequencies(width)[None, :]
    embed = jnp.concatenate([jnp.sin(angles), jnp.cos(angles)], axis=1)
    normalize = call(
        norm_kernel,
        (arr((rows, width), F32), arr((rows, half), F32)),
        [SMEM] + [VMEM] * 2,
        flops=10 * rows * width,
        byts=8 * rows * width,
    )
    normed0, diff0 = normalize(coef, latents, noise)
    normed1, diff1 = normalize(coef, other_latents, other_noise)

    wa = call(
        functools.partial(join_kernel, unit),
        arr((two, half), BF),
        [VMEM] * 2 + [ANY],
        byts=8 * unit * half,
    )(own, z1, diff0)
    wa1 = to(wa, 1)
    wb, gain_tile = call(
        functools.partial(join_gain_kernel, unit),
        (arr((two + 16, half), BF), arr((16, half), BF)),
        [VMEM] * 4 + [ANY],
        byts=8 * unit * half,
    )(own, z1, z2, z3, diff1)
    wb1 = to(wb, 2)
    gain_x, gain_xy = to(gain_tile, 1), to(gain_tile, 3)
    pair = call(pair_kernel, arr((four, half), BF), [VMEM] * 2, byts=16 * unit * half)
    wa2 = to(pair(wa, wa1), 2)
    wb2 = to(pair(wb, wb1), 1)
    gain_y = wb1[two:]
    act, slope = call(
        functools.partial(act_kernel, unit),
        (arr((both, width), BF), arr((both, width), F32)),
        [VMEM] * 7,
        [pltpu.VMEM((16, 128), F32), pltpu.VMEM((1, width), F32)],
        flops=20 * both * width,
        byts=8 * both * width,
    )(embed, gain_tile, gain_x, gain_y, gain_xy, normed0, normed1)

    send_a, send_b, keep_a, keep_b, keep_g = call(
        functools.partial(mix_kernel, 1.0 / math.sqrt(total_rows), unit),
        (
            arr((four + 16, half), BF),
            arr((four, half), BF),
            arr((four, half), F32),
            arr((four, half), F32),
            arr((8, half), F32),
        ),
        [VMEM] * 10,
        [
            pltpu.VMEM((width, half), BF),
            pltpu.VMEM((width, half), F32),
            pltpu.VMEM((both, half), BF),
            pltpu.VMEM((16, 128), F32),
        ],
        flops=6 * both * width * half,
        byts=6 * both * width,
    )(act, slope, diff0, diff1, wa, wa1, wa2, wb, wb1, wb2)

    got_a, got_b = to(send_a, 1), to(send_b, 2)
    send_a, own_a, own_g = call(
        functools.partial(fold_a_kernel, unit),
        (arr((two + 16, half), BF), arr((two, half), F32), arr((8, half), F32)),
        [VMEM] * 3,
        byts=8 * four * half,
    )(keep_a, keep_g, got_a)
    got_a = to(send_a, 2)
    send_b, own_b = call(
        functools.partial(fold_b_kernel, unit),
        (arr((two, half), BF), arr((two, half), F32)),
        [VMEM] * 2,
        byts=8 * four * half,
    )(keep_b, got_b)
    got_b = to(send_b, 1)
    send1, mine, line = call(
        functools.partial(turn_a_kernel, unit),
        (arr((unit + 16, half), BF), arr((unit, half), F32), arr((8, half), F32)),
        [VMEM] * 3,
        byts=8 * two * half,
    )(own_a, own_g, got_a)
    h1 = to(send1, 4)
    send2, send3 = call(
        functools.partial(turn_b_kernel, unit),
        (arr((unit + 16, half), BF), arr((unit + 16, half), BF)),
        [VMEM] * 3,
        byts=8 * two * half,
    )(own_b, got_b, line)
    h2, h3 = to(send2, 8), to(send3, 12)
    mine = call(
        functools.partial(last_kernel, unit),
        arr((unit + 8, half), F32),
        [VMEM] * 5,
        byts=16 * unit * half,
    )(mine, line, h1, h2, h3)
    theirs = across(mine)
    flat = arr((unit, width), F32)
    thin = arr((1, unit), F32)
    *weights, ng, ngm, ngs = call(
        functools.partial(adam_kernel, unit, half),
        (flat, flat, flat, thin, thin, thin),
        [VMEM] * 8,
        byts=24 * unit * width,
    )(
        mine, theirs, master_weight, weight_moment, weight_second,
        *(x.reshape(1, unit) for x in (norm_gain, gain_moment, gain_second)),
    )
    return (*weights, ng.reshape(unit), ngm.reshape(unit), ngs.reshape(unit))


def body(latents, *rest):
    rows, width = latents.shape
    unit = rest[2].shape[0]
    paired = (
        lax.axis_size("shard") == 16
        and lax.axis_size("replica") == 2
        and unit % 16 == 0
        and unit <= 128
        and width % 256 == 0
        and width >= 1024
        and rows % 16 == 0
        and VOX % (2 * rows) == 0
    )
    return (paired_body if paired else general_body)(latents, *rest)


def solution(mesh):
    rows = P(AXES, None)
    block = P("shard", None)
    line = P("shard")
    return jax.shard_map(
        body,
        mesh=mesh,
        in_specs=(rows, rows, P(), block, line, block, block, line, line),
        out_specs=(block, block, block, line, line, line),
        check_vma=False,
    )
```

```python
import functools
import math

import jax
import jax.numpy as jnp
from jax import lax
from jax.experimental import pallas as pl
from jax.experimental.pallas import tpu as pltpu
from jax.sharding import PartitionSpec as P

VOX = 512
AXES = ("shard", "replica")
BF = jnp.bfloat16
F32 = jnp.float32

bias_first = 0.9999734386011124
bias_second = 0.095207852886291


def adam_step(param, grad, moment, second):
    new_moment = 0.9 * moment + 0.1 * grad
    new_second = 0.999 * second + 0.001 * grad * grad
    update = new_moment / bias_first / (jnp.sqrt(new_second / bias_second) + 1e-08)
    return (param - 0.05 * update, new_moment, new_second)


def frequencies(width):
    half = width // 2
    return jnp.exp(-(2.0 * jnp.arange(half, dtype=F32) / width) * math.log(10000.0))


def noise_level(step_time):
    return jnp.cos((step_time / 1000.0 + 0.008) / 1.008 * (math.pi / 2)) ** 2


def general_body(
    latents, noise, timesteps, master_weight, norm_gain, weight_moment, weight_second, gain_moment, gain_second
):
    rows, width = latents.shape
    shard_count = lax.axis_size("shard")
    replica_count = lax.axis_size("replica")
    total_rows = rows * shard_count * replica_count
    block_index = lax.axis_index("shard") * replica_count + lax.axis_index("replica")
    row_ids = block_index * rows + jnp.arange(rows, dtype=jnp.int32)
    step_time = timesteps[row_ids // VOX].astype(F32)
    level = noise_level(step_time)
    noisy = (
        jnp.sqrt(level)[:, None] * latents.astype(F32)
        + jnp.sqrt(1.0 - level)[:, None] * noise.astype(F32)
    )
    angles = step_time[:, None] * frequencies(width)[None, :]
    embed = jnp.concatenate([jnp.sin(angles), jnp.cos(angles)], axis=1)
    mean = jnp.mean(noisy, axis=1, keepdims=True)
    var = jnp.mean((noisy - mean) ** 2, axis=1, keepdims=True)
    normed = (noisy - mean) / jnp.sqrt(var + 1e-05)
    full_gain = lax.all_gather(norm_gain, "shard", axis=0, tiled=True)
    hidden = normed * full_gain[None, :] + embed
    act = jax.nn.silu(hidden).astype(BF)
    mixing = lax.all_gather(master_weight.astype(BF), "shard", axis=0, tiled=True)
    scale = 1.0 / math.sqrt(total_rows)
    predicted = noisy + jnp.dot(act, mixing, preferred_element_type=F32)
    grad_out = ((predicted - noise.astype(F32)) * scale).astype(BF)
    grad_act = lax.dot_general(
        grad_out, mixing, (((1,), (1,)), ((), ())), preferred_element_type=F32
    )
    weight_share = lax.psum_scatter(
        lax.dot_general(act, grad_out, (((0,), (0,)), ((), ())), preferred_element_type=F32),
        "shard",
        scatter_dimension=0,
        tiled=True,
    )
    sig = jax.nn.sigmoid(hidden)
    grad_hidden = grad_act * (sig * (1.0 + hidden * (1.0 - sig)))
    gain_local = jnp.sum(grad_hidden * normed, axis=0)
    gain_share = lax.psum_scatter(gain_local, "shard", scatter_dimension=0, tiled=True)
    weight_grad, gain_grad = lax.psum((weight_share, gain_share), "replica")
    return (
        *adam_step(master_weight, weight_grad, weight_moment, weight_second),
        *adam_step(norm_gain, gain_grad, gain_moment, gain_second),
    )


VMEM = pl.BlockSpec(memory_space=pltpu.VMEM)
ANY = pl.BlockSpec(memory_space=pl.ANY)
HBM = pl.BlockSpec(memory_space=pltpu.HBM)
SMEM = pl.BlockSpec(memory_space=pltpu.SMEM)


def split(x, parts):
    out = []
    for _ in range(parts):
        top = x.astype(BF).astype(F32)
        out.append(top)
        x = x - top
    return out


def stack_rows(pieces, shape):
    row = lax.broadcasted_iota(jnp.int32, shape, 0)
    tile = jnp.zeros(shape, F32)
    for i, piece in enumerate(pieces):
        tile = jnp.where(row == i, jnp.broadcast_to(piece, shape), tile)
    return tile


def pack_kernel(w_ref, gain_ref, out_ref, part_ref, sem):
    unit, half = part_ref.shape
    col = pl.ds(pl.multiple_of(lax.axis_index("replica") * half, 128), half)
    copy = pltpu.make_async_copy(w_ref.at[:, col], part_ref, sem)
    copy.start()
    out_ref[unit:, :] = jnp.zeros((16, half), BF)
    gain = stack_rows(split(gain_ref[...], 3), (16, unit))
    out_ref[unit:, :unit] = gain.astype(BF)
    copy.wait()
    out_ref[:unit, :] = part_ref[...].astype(BF)


def join_kernel(unit, own, z1, z2, z3, wa, wb, tile):
    tile[...] = jnp.zeros_like(tile)
    for i, z in enumerate((own, z1, z2, z3)):
        to = wa if i < 2 else wb
        to[(i % 2) * unit : (i % 2 + 1) * unit, :] = z[:unit, :]
        tile[:, 128 * i : 128 * i + 128] = z[unit:, :128]
    wa[2 * unit :, :] = tile[...]
    wb[2 * unit :, :] = tile[...]


def pair_kernel(first, second, after, out):
    n = out.shape[0] // 2
    out[:n, :] = first[:n, :]
    out[n:, :] = second[:n, :]


def act_kernel(
    unit, coef_ref, embed_ref, t0, t1, t2, t3, l0, n0, l1, n1, after_a, after_b,
    act_ref, slope_ref, diff_ref, slots, gain_ref,
):
    me = lax.axis_index("shard")
    width = act_ref.shape[1]
    half = width // 2
    for kp, (t, first) in enumerate(((t0, 0), (t1, 2 * unit), (t2, 2 * unit), (t3, 0))):
        x = t[first : first + 16, :].astype(F32)
        line = x[0:1, :] + x[1:2, :] + x[2:3, :]
        for kz in range(4):
            slots[4 * kz + kp : 4 * kz + kp + 1, :] = line[:, 128 * kz : 128 * kz + 128]
    for i in range(16):
        gain_ref[:, i * unit : (i + 1) * unit] = slots[pl.ds(me ^ i, 1), :unit]
    gain = gain_ref[...]
    embed = embed_ref[...]
    col = pl.ds(pl.multiple_of(lax.axis_index("replica") * half, 128), half)
    a, b = coef_ref[0], coef_ref[1]
    tile = 32
    for part, (l_ref, n_ref) in enumerate(((l0, n0), (l1, n1))):
        rows = l_ref.shape[0]

        def step(i, carry, l_ref=l_ref, n_ref=n_ref, base=part * rows):
            at = pl.ds(pl.multiple_of(i * tile, tile), tile)
            to = pl.ds(pl.multiple_of(base + i * tile, tile), tile)
            noisy = a * l_ref[at, :].astype(F32) + b * n_ref[at, :].astype(F32)
            mean = jnp.sum(noisy, axis=1, keepdims=True) * (1.0 / width)
            cent = noisy - mean
            var = jnp.sum(cent * cent, axis=1, keepdims=True) * (1.0 / width)
            normed = cent * (1.0 / jnp.sqrt(var + 1e-05))
            nh = n_ref[at, col].astype(F32)
            diff_ref[to, :] = (a * l_ref[at, col].astype(F32) + b * nh) - nh
            hidden = normed * gain + embed
            sig = 0.5 * jnp.tanh(0.5 * hidden) + 0.5
            act = hidden * sig
            act_ref[to, :] = act.astype(BF)
            slope_ref[to, :] = (sig + act * (1.0 - sig)) * normed
            return carry

        lax.fori_loop(0, rows // tile, step, 0)


def mix_kernel(
    scale, unit, act_ref, slope_ref, diff_ref, wa, wa1, wa2, wb, wb1, wb2,
    send_a, send_b, keep_a, keep_b, keep_g, w_ref, wg_ref, gout_ref, slots,
):
    me = lax.axis_index("shard")

    def place(kz, kp):
        return pl.ds(pl.multiple_of((me ^ (kz * 4 + kp)) * unit, 16), unit)

    def rows(i):
        return pl.ds(i * unit, unit)

    for k in range(2):
        w_ref[place(k, 0), :] = wa[rows(k), :]
        w_ref[place(k, 1), :] = wa1[rows(k), :]
        w_ref[place(k, 2), :] = wa2[rows(k), :]
        w_ref[place(k, 3), :] = wa2[rows(2 + k), :]
        w_ref[place(2 + k, 0), :] = wb[rows(k), :]
        w_ref[place(2 + k, 2), :] = wb1[rows(k), :]
        w_ref[place(2 + k, 1), :] = wb2[rows(k), :]
        w_ref[place(2 + k, 3), :] = wb2[rows(2 + k), :]
    product = jnp.dot(act_ref[...], w_ref[...], preferred_element_type=F32)
    gout_ref[...] = ((diff_ref[...] + product) * scale).astype(BF)
    grad_act = lax.dot_general(
        gout_ref[...], w_ref[...], (((1,), (1,)), ((), ())), preferred_element_type=F32
    )
    part = jnp.sum(grad_act * slope_ref[...], axis=0, keepdims=True)
    wg_ref[...] = lax.dot_general(
        act_ref[...], gout_ref[...], (((0,), (0,)), ((), ())), preferred_element_type=F32
    )
    half = wg_ref.shape[1]
    slots[...] = jnp.zeros_like(slots)
    for i in range(16):
        slots[pl.ds(me ^ i, 1), :unit] = part[:, i * unit : (i + 1) * unit]
    lines = [
        jnp.concatenate([slots[4 * kz + kp : 4 * kz + kp + 1, :] for kz in range(4)], axis=1)
        for kp in range(4)
    ]
    keep_g[...] = jnp.zeros_like(keep_g)
    keep_g[0:1, :512] = lines[0]
    keep_g[1:2, :512] = lines[2]
    for k in range(2):
        send_a[rows(k), :] = wg_ref[place(k, 1), :].astype(BF)
        send_a[rows(2 + k), :] = wg_ref[place(k, 3), :].astype(BF)
        keep_a[rows(k), :] = wg_ref[place(k, 0), :]
        keep_a[rows(2 + k), :] = wg_ref[place(k, 2), :]
        send_b[rows(k), :] = wg_ref[place(2 + k, 2), :].astype(BF)
        send_b[rows(2 + k), :] = wg_ref[place(2 + k, 3), :].astype(BF)
        keep_b[rows(k), :] = wg_ref[place(2 + k, 0), :]
        keep_b[rows(2 + k), :] = wg_ref[place(2 + k, 1), :]
    send_a[4 * unit :, :] = jnp.zeros((16, half), BF)
    send_a[4 * unit :, :512] = stack_rows(split(lines[1], 2) + split(lines[3], 2), (16, 512)).astype(BF)


def fold_a_kernel(unit, keep_a, keep_g, got, send, own, own_g):
    two = 2 * unit
    send[:two, :] = (keep_a[two:, :] + got[two : 2 * two, :].astype(F32)).astype(BF)
    extra = got[2 * two :, :].astype(F32)
    own_g[...] = jnp.zeros_like(own_g)
    own_g[0:1, :] = keep_g[0:1, :] + (extra[0:1, :] + extra[1:2, :])
    line = keep_g[1:2, :] + (extra[2:3, :] + extra[3:4, :])
    send[two:, :] = stack_rows(split(line, 2), (16, line.shape[1])).astype(BF)
    own[...] = keep_a[:two, :] + got[:two, :].astype(F32)


def fold_b_kernel(unit, keep_b, got, send, own):
    two = 2 * unit
    send[...] = (keep_b[two:, :] + got[two:, :].astype(F32)).astype(BF)
    own[...] = keep_b[:two, :] + got[:two, :].astype(F32)


def turn_a_kernel(unit, own, own_g, got, send1, mine, line_ref):
    two = 2 * unit
    half = own.shape[1]
    extra = got[two:, :].astype(F32)
    line = own_g[0:1, :] + (extra[0:1, :] + extra[1:2, :])
    send1[:unit, :] = (own[unit:, :] + got[unit:two, :].astype(F32)).astype(BF)
    send1[unit:, :] = jnp.zeros((16, half), BF)
    send1[unit:, :128] = stack_rows(split(line[:, 128:256], 2), (16, 128)).astype(BF)
    mine[...] = own[:unit, :] + got[:unit, :].astype(F32)
    line_ref[...] = jnp.zeros_like(line_ref)
    line_ref[0:1, :] = line


def turn_b_kernel(unit, own, got, line_ref, send2, send3):
    half = own.shape[1]
    total = own[...] + got[...].astype(F32)
    for k, send in ((2, send2), (3, send3)):
        send[:unit, :] = total[(k - 2) * unit : (k - 1) * unit, :].astype(BF)
        send[unit:, :] = jnp.zeros((16, half), BF)
        piece = line_ref[0:1, 128 * k : 128 * k + 128]
        send[unit:, :128] = stack_rows(split(piece, 2), (16, 128)).astype(BF)


def last_kernel(unit, mine, line_ref, h1, h2, h3, out_ref):
    total = mine[...]
    line = line_ref[0:1, :128]
    for h in (h1, h2, h3):
        total = total + h[:unit, :].astype(F32)
        extra = h[unit:, :128].astype(F32)
        line = line + (extra[0:1, :] + extra[1:2, :])
    out_ref[:unit, :] = total
    out_ref[unit:, :] = jnp.zeros((8, total.shape[1]), F32)
    out_ref[unit : unit + 1, :128] = line


def adam_kernel(unit, half, mine, theirs, w, wm, ws, g, gm, gs, nw, nwm, nws, ng, ngm, ngs):
    core = lax.axis_index("replica")
    for ref, side in ((mine, core), (theirs, 1 - core)):
        col = pl.ds(pl.multiple_of(side * half, 128), half)
        nw[:, col], nwm[:, col], nws[:, col] = adam_step(
            w[:, col], ref[:unit, :], wm[:, col], ws[:, col]
        )
    line = mine[unit : unit + 1, :unit] + theirs[unit : unit + 1, :unit]
    ng[...], ngm[...], ngs[...] = adam_step(g[...], line, gm[...], gs[...])


def paired_body(
    latents, noise, timesteps, master_weight, norm_gain, weight_moment, weight_second, gain_moment, gain_second
):
    rows, width = latents.shape
    unit = master_weight.shape[0]
    shards, cores = lax.axis_size("shard"), lax.axis_size("replica")
    total_rows = rows * shards * cores
    half = width // 2
    both = rows * cores
    me = lax.axis_index("shard")

    def to(x, k):
        pairs = [(i * cores + c, (i ^ k) * cores + c) for i in range(shards) for c in range(cores)]
        return lax.ppermute(x, AXES, pairs)

    def across(x):
        pairs = [(i * cores + c, i * cores + 1 - c) for i in range(shards) for c in range(cores)]
        return lax.ppermute(x, AXES, pairs)

    def call(kernel, outs, specs, scratch=(), flops=0, byts=0):
        return pl.pallas_call(
            kernel,
            out_shape=outs,
            in_specs=specs,
            out_specs=jax.tree.map(lambda _: VMEM, outs),
            scratch_shapes=list(scratch),
            compiler_params=pltpu.CompilerParams(vmem_limit_bytes=40 << 20),
            cost_estimate=pl.CostEstimate(flops=flops, bytes_accessed=byts, transcendentals=0),
        )

    arr = jax.ShapeDtypeStruct
    two, four = 2 * unit, 4 * unit

    own = call(
        pack_kernel,
        arr((unit + 16, half), BF),
        [HBM, VMEM],
        [pltpu.VMEM((unit, half), F32), pltpu.SemaphoreType.DMA],
        byts=6 * unit * half,
    )(master_weight, norm_gain.reshape(1, unit))
    z1, z2, z3 = to(own, 4), to(own, 8), to(own, 12)
    wa, wb, tile = call(
        functools.partial(join_kernel, unit),
        (arr((two + 16, half), BF), arr((two + 16, half), BF), arr((16, half), BF)),
        [VMEM] * 4,
        byts=16 * unit * half,
    )(own, z1, z2, z3)
    wa1, wb1 = to(wa, 1), to(wb, 2)
    far = to(tile, 3)
    pair = call(pair_kernel, arr((four, half), BF), [VMEM] * 2 + [ANY], byts=16 * unit * half)
    pair_a, pair_b = pair(wa, wa1, far), pair(wb, wb1, far)
    wa2, wb2 = to(pair_a, 2), to(pair_b, 1)

    other_latents, other_noise = across(latents), across(noise)
    step_time = lax.dynamic_slice(timesteps, (me * cores * rows // VOX,), (1,)).astype(F32)
    level = noise_level(step_time)
    coef = jnp.concatenate([jnp.sqrt(level), jnp.sqrt(1.0 - level)])
    angles = step_time[:, None] * frequencies(width)[None, :]
    embed = jnp.concatenate([jnp.sin(angles), jnp.cos(angles)], axis=1)
    act, slope, diff = call(
        functools.partial(act_kernel, unit),
        (arr((both, width), BF), arr((both, width), F32), arr((both, half), F32)),
        [SMEM] + [VMEM] * 9 + [ANY] * 2,
        [pltpu.VMEM((16, 128), F32), pltpu.VMEM((1, width), F32)],
        byts=28 * both * width,
    )(coef, embed, tile, wa1, wb1, far, latents, noise, other_latents, other_noise, pair_a, pair_b)

    send_a, send_b, keep_a, keep_b, keep_g = call(
        functools.partial(mix_kernel, 1.0 / math.sqrt(total_rows), unit),
        (
            arr((four + 16, half), BF),
            arr((four, half), BF),
            arr((four, half), F32),
            arr((four, half), F32),
            arr((8, half), F32),
        ),
        [VMEM] * 9,
        [
            pltpu.VMEM((width, half), BF),
            pltpu.VMEM((width, half), F32),
            pltpu.VMEM((both, half), BF),
            pltpu.VMEM((16, 128), F32),
        ],
        flops=6 * both * width * half,
        byts=6 * both * width,
    )(act, slope, diff, wa, wa1, wa2, wb, wb1, wb2)

    got_a, got_b = to(send_a, 1), to(send_b, 2)
    send_a, own_a, own_g = call(
        functools.partial(fold_a_kernel, unit),
        (arr((two + 16, half), BF), arr((two, half), F32), arr((8, half), F32)),
        [VMEM] * 3,
        byts=8 * four * half,
    )(keep_a, keep_g, got_a)
    got_a = to(send_a, 2)
    send_b, own_b = call(
        functools.partial(fold_b_kernel, unit),
        (arr((two, half), BF), arr((two, half), F32)),
        [VMEM] * 2,
        byts=8 * four * half,
    )(keep_b, got_b)
    got_b = to(send_b, 1)
    send1, mine, line = call(
        functools.partial(turn_a_kernel, unit),
        (arr((unit + 16, half), BF), arr((unit, half), F32), arr((8, half), F32)),
        [VMEM] * 3,
        byts=8 * two * half,
    )(own_a, own_g, got_a)
    h1 = to(send1, 4)
    send2, send3 = call(
        functools.partial(turn_b_kernel, unit),
        (arr((unit + 16, half), BF), arr((unit + 16, half), BF)),
        [VMEM] * 3,
        byts=8 * two * half,
    )(own_b, got_b, line)
    h2, h3 = to(send2, 8), to(send3, 12)
    mine = call(
        functools.partial(last_kernel, unit),
        arr((unit + 8, half), F32),
        [VMEM] * 5,
        byts=16 * unit * half,
    )(mine, line, h1, h2, h3)
    theirs = across(mine)
    flat = arr((unit, width), F32)
    thin = arr((1, unit), F32)
    *weights, ng, ngm, ngs = call(
        functools.partial(adam_kernel, unit, half),
        (flat, flat, flat, thin, thin, thin),
        [VMEM] * 8,
        byts=24 * unit * width,
    )(
        mine, theirs, master_weight, weight_moment, weight_second,
        *(x.reshape(1, unit) for x in (norm_gain, gain_moment, gain_second)),
    )
    return (*weights, ng.reshape(unit), ngm.reshape(unit), ngs.reshape(unit))


def body(latents, *rest):
    rows, width = latents.shape
    unit = rest[2].shape[0]
    paired = (
        lax.axis_size("shard") == 16
        and lax.axis_size("replica") == 2
        and unit % 16 == 0
        and unit <= 128
        and width % 256 == 0
        and width >= 1024
        and rows % 16 == 0
        and VOX % (2 * rows) == 0
    )
    return (paired_body if paired else general_body)(latents, *rest)


def solution(mesh):
    rows = P(AXES, None)
    block = P("shard", None)
    line = P("shard")
    return jax.shard_map(
        body,
        mesh=mesh,
        in_specs=(rows, rows, P(), block, line, block, block, line, line),
        out_specs=(block, block, block, line, line, line),
        check_vma=False,
    )
```

```python
import functools
import math

import jax
import jax.numpy as jnp
from jax import lax
from jax.experimental import pallas as pl
from jax.experimental.pallas import tpu as pltpu
from jax.sharding import PartitionSpec as P

VOX = 512
AXES = ("shard", "replica")
BF = jnp.bfloat16
F32 = jnp.float32

bias_first = 0.9999734386011124
bias_second = 0.095207852886291


def adam_step(param, grad, moment, second):
    new_moment = 0.9 * moment + 0.1 * grad
    new_second = 0.999 * second + 0.001 * grad * grad
    update = new_moment / bias_first / (jnp.sqrt(new_second / bias_second) + 1e-08)
    return (param - 0.05 * update, new_moment, new_second)


def frequencies(width):
    half = width // 2
    return jnp.exp(-(2.0 * jnp.arange(half, dtype=F32) / width) * math.log(10000.0))


def noise_level(step_time):
    return jnp.cos((step_time / 1000.0 + 0.008) / 1.008 * (math.pi / 2)) ** 2


def general_body(
    latents, noise, timesteps, master_weight, norm_gain, weight_moment, weight_second, gain_moment, gain_second
):
    rows, width = latents.shape
    shard_count = lax.axis_size("shard")
    replica_count = lax.axis_size("replica")
    total_rows = rows * shard_count * replica_count
    block_index = lax.axis_index("shard") * replica_count + lax.axis_index("replica")
    row_ids = block_index * rows + jnp.arange(rows, dtype=jnp.int32)
    step_time = timesteps[row_ids // VOX].astype(F32)
    level = noise_level(step_time)
    noisy = (
        jnp.sqrt(level)[:, None] * latents.astype(F32)
        + jnp.sqrt(1.0 - level)[:, None] * noise.astype(F32)
    )
    angles = step_time[:, None] * frequencies(width)[None, :]
    embed = jnp.concatenate([jnp.sin(angles), jnp.cos(angles)], axis=1)
    mean = jnp.mean(noisy, axis=1, keepdims=True)
    var = jnp.mean((noisy - mean) ** 2, axis=1, keepdims=True)
    normed = (noisy - mean) / jnp.sqrt(var + 1e-05)
    full_gain = lax.all_gather(norm_gain, "shard", axis=0, tiled=True)
    hidden = normed * full_gain[None, :] + embed
    act = jax.nn.silu(hidden).astype(BF)
    mixing = lax.all_gather(master_weight.astype(BF), "shard", axis=0, tiled=True)
    scale = 1.0 / math.sqrt(total_rows)
    predicted = noisy + jnp.dot(act, mixing, preferred_element_type=F32)
    grad_out = ((predicted - noise.astype(F32)) * scale).astype(BF)
    grad_act = lax.dot_general(
        grad_out, mixing, (((1,), (1,)), ((), ())), preferred_element_type=F32
    )
    weight_share = lax.psum_scatter(
        lax.dot_general(act, grad_out, (((0,), (0,)), ((), ())), preferred_element_type=F32),
        "shard",
        scatter_dimension=0,
        tiled=True,
    )
    sig = jax.nn.sigmoid(hidden)
    grad_hidden = grad_act * (sig * (1.0 + hidden * (1.0 - sig)))
    gain_local = jnp.sum(grad_hidden * normed, axis=0)
    gain_share = lax.psum_scatter(gain_local, "shard", scatter_dimension=0, tiled=True)
    weight_grad, gain_grad = lax.psum((weight_share, gain_share), "replica")
    return (
        *adam_step(master_weight, weight_grad, weight_moment, weight_second),
        *adam_step(norm_gain, gain_grad, gain_moment, gain_second),
    )


VMEM = pl.BlockSpec(memory_space=pltpu.VMEM)
ANY = pl.BlockSpec(memory_space=pl.ANY)
HBM = pl.BlockSpec(memory_space=pltpu.HBM)
SMEM = pl.BlockSpec(memory_space=pltpu.SMEM)


def split(x, parts):
    out = []
    for _ in range(parts):
        top = x.astype(BF).astype(F32)
        out.append(top)
        x = x - top
    return out


def stack_rows(pieces, shape):
    row = lax.broadcasted_iota(jnp.int32, shape, 0)
    tile = jnp.zeros(shape, F32)
    for i, piece in enumerate(pieces):
        tile = jnp.where(row == i, jnp.broadcast_to(piece, shape), tile)
    return tile


def pack_kernel(w_ref, gain_hbm, out_ref, part_ref, gain_ref, sem, gain_sem):
    unit, half = part_ref.shape
    col = pl.ds(pl.multiple_of(lax.axis_index("replica") * half, 128), half)
    copy = pltpu.make_async_copy(w_ref.at[:, col], part_ref, sem)
    copy.start()
    gain_copy = pltpu.make_async_copy(gain_hbm, gain_ref, gain_sem)
    gain_copy.start()
    out_ref[unit:, :] = jnp.zeros((16, half), BF)
    gain_copy.wait()
    gain = stack_rows(split(gain_ref[...], 3), (16, unit))
    out_ref[unit:, :unit] = gain.astype(BF)
    copy.wait()
    out_ref[:unit, :] = part_ref[...].astype(BF)


def join_kernel(unit, own, z1, z2, z3, wa, wb, tile):
    tile[...] = jnp.zeros_like(tile)
    for i, z in enumerate((own, z1, z2, z3)):
        to = wa if i < 2 else wb
        to[(i % 2) * unit : (i % 2 + 1) * unit, :] = z[:unit, :]
        tile[:, 128 * i : 128 * i + 128] = z[unit:, :128]
    wa[2 * unit :, :] = tile[...]
    wb[2 * unit :, :] = tile[...]


def pair_kernel(first, second, after, out):
    n = out.shape[0] // 2
    out[:n, :] = first[:n, :]
    out[n:, :] = second[:n, :]


def act_kernel(
    unit, coef_ref, embed_ref, t0, t1, t2, t3, l0, n0, l1, n1, after_a, after_b,
    act_ref, slope_ref, diff_ref, slots, gain_ref,
):
    me = lax.axis_index("shard")
    width = act_ref.shape[1]
    half = width // 2
    for kp, (t, first) in enumerate(((t0, 0), (t1, 2 * unit), (t2, 2 * unit), (t3, 0))):
        x = t[first : first + 16, :].astype(F32)
        line = x[0:1, :] + x[1:2, :] + x[2:3, :]
        for kz in range(4):
            slots[4 * kz + kp : 4 * kz + kp + 1, :] = line[:, 128 * kz : 128 * kz + 128]
    for i in range(16):
        gain_ref[:, i * unit : (i + 1) * unit] = slots[pl.ds(me ^ i, 1), :unit]
    gain = gain_ref[...]
    embed = embed_ref[...]
    col = pl.ds(pl.multiple_of(lax.axis_index("replica") * half, 128), half)
    a, b = coef_ref[0], coef_ref[1]
    tile = 32
    for part, (l_ref, n_ref) in enumerate(((l0, n0), (l1, n1))):
        rows = l_ref.shape[0]

        def step(i, carry, l_ref=l_ref, n_ref=n_ref, base=part * rows):
            at = pl.ds(pl.multiple_of(i * tile, tile), tile)
            to = pl.ds(pl.multiple_of(base + i * tile, tile), tile)
            noisy = a * l_ref[at, :].astype(F32) + b * n_ref[at, :].astype(F32)
            mean = jnp.sum(noisy, axis=1, keepdims=True) * (1.0 / width)
            cent = noisy - mean
            var = jnp.sum(cent * cent, axis=1, keepdims=True) * (1.0 / width)
            normed = cent * (1.0 / jnp.sqrt(var + 1e-05))
            nh = n_ref[at, col].astype(F32)
            diff_ref[to, :] = (a * l_ref[at, col].astype(F32) + b * nh) - nh
            hidden = normed * gain + embed
            sig = 0.5 * jnp.tanh(0.5 * hidden) + 0.5
            act = hidden * sig
            act_ref[to, :] = act.astype(BF)
            slope_ref[to, :] = (sig + act * (1.0 - sig)) * normed
            return carry

        lax.fori_loop(0, rows // tile, step, 0)


def mix_kernel(
    scale, unit, act_ref, diff_ref, wa, wa1, wa2, wb, wb1, wb2,
    send_a, send_b, keep_a, keep_b, w_ref, gout_ref, wg_ref,
):
    me = lax.axis_index("shard")

    def place(kz, kp):
        return pl.ds(pl.multiple_of((me ^ (kz * 4 + kp)) * unit, 16), unit)

    def rows(i):
        return pl.ds(i * unit, unit)

    for k in range(2):
        w_ref[place(k, 0), :] = wa[rows(k), :]
        w_ref[place(k, 1), :] = wa1[rows(k), :]
        w_ref[place(k, 2), :] = wa2[rows(k), :]
        w_ref[place(k, 3), :] = wa2[rows(2 + k), :]
        w_ref[place(2 + k, 0), :] = wb[rows(k), :]
        w_ref[place(2 + k, 2), :] = wb1[rows(k), :]
        w_ref[place(2 + k, 1), :] = wb2[rows(k), :]
        w_ref[place(2 + k, 3), :] = wb2[rows(2 + k), :]
    product = jnp.dot(act_ref[...], w_ref[...], preferred_element_type=F32)
    gout_ref[...] = ((diff_ref[...] + product) * scale).astype(BF)
    wg_ref[...] = lax.dot_general(
        act_ref[...], gout_ref[...], (((0,), (0,)), ((), ())), preferred_element_type=F32
    )
    for k in range(2):
        send_a[rows(k), :] = wg_ref[place(k, 1), :].astype(BF)
        send_a[rows(2 + k), :] = wg_ref[place(k, 3), :].astype(BF)
        keep_a[rows(k), :] = wg_ref[place(k, 0), :]
        keep_a[rows(2 + k), :] = wg_ref[place(k, 2), :]
        send_b[rows(k), :] = wg_ref[place(2 + k, 2), :].astype(BF)
        send_b[rows(2 + k), :] = wg_ref[place(2 + k, 3), :].astype(BF)
        keep_b[rows(k), :] = wg_ref[place(2 + k, 0), :]
        keep_b[rows(2 + k), :] = wg_ref[place(2 + k, 1), :]


def gain_kernel(unit, gout_ref, w_ref, slope_ref, keep, send, slots):
    me = lax.axis_index("shard")
    grad_act = lax.dot_general(
        gout_ref[...], w_ref[...], (((1,), (1,)), ((), ())), preferred_element_type=F32
    )
    part = jnp.sum(grad_act * slope_ref[...], axis=0, keepdims=True)
    slots[...] = jnp.zeros_like(slots)
    for i in range(16):
        slots[pl.ds(me ^ i, 1), :unit] = part[:, i * unit : (i + 1) * unit]
    for kp in range(4):
        out = send if kp % 2 else keep
        for kz in range(4):
            out[kp // 2 : kp // 2 + 1, 128 * kz : 128 * kz + 128] = slots[4 * kz + kp : 4 * kz + kp + 1, :]


def fold_a_kernel(unit, keep_a, got, keep_g, got_g, send, own, send_g, own_g):
    two = 2 * unit
    own_g[...] = keep_g[0:1, :] + got_g[0:1, :]
    send_g[...] = keep_g[1:2, :] + got_g[1:2, :]
    send[...] = (keep_a[two:, :] + got[two:, :].astype(F32)).astype(BF)
    own[...] = keep_a[:two, :] + got[:two, :].astype(F32)


def fold_b_kernel(unit, keep_b, got, send, own):
    two = 2 * unit
    send[...] = (keep_b[two:, :] + got[two:, :].astype(F32)).astype(BF)
    own[...] = keep_b[:two, :] + got[:two, :].astype(F32)


def turn_a_kernel(unit, own, got, own_g, got_g, send1, mine, line_ref):
    half = own.shape[1]
    line = own_g[...] + got_g[...]
    send1[:unit, :] = (own[unit:, :] + got[unit:, :].astype(F32)).astype(BF)
    send1[unit:, :] = jnp.zeros((16, half), BF)
    send1[unit:, :128] = stack_rows(split(line[:, 128:256], 2), (16, 128)).astype(BF)
    mine[...] = own[:unit, :] + got[:unit, :].astype(F32)
    line_ref[...] = jnp.zeros_like(line_ref)
    line_ref[0:1, :512] = line


def turn_b_kernel(unit, own, got, line_ref, send2, send3):
    half = own.shape[1]
    total = own[...] + got[...].astype(F32)
    for k, send in ((2, send2), (3, send3)):
        send[:unit, :] = total[(k - 2) * unit : (k - 1) * unit, :].astype(BF)
        send[unit:, :] = jnp.zeros((16, half), BF)
        piece = line_ref[0:1, 128 * k : 128 * k + 128]
        send[unit:, :128] = stack_rows(split(piece, 2), (16, 128)).astype(BF)


def last_kernel(unit, mine, line_ref, h1, h2, h3, out_ref):
    total = mine[...]
    line = line_ref[0:1, :128]
    for h in (h1, h2, h3):
        total = total + h[:unit, :].astype(F32)
        extra = h[unit:, :128].astype(F32)
        line = line + (extra[0:1, :] + extra[1:2, :])
    out_ref[:unit, :] = total
    out_ref[unit:, :] = jnp.zeros((8, total.shape[1]), F32)
    out_ref[unit : unit + 1, :128] = line


def adam_kernel(unit, half, mine, theirs, w, wm, ws, g, gm, gs, nw, nwm, nws, ng, ngm, ngs):
    core = lax.axis_index("replica")
    for ref, side in ((mine, core), (theirs, 1 - core)):
        col = pl.ds(pl.multiple_of(side * half, 128), half)
        nw[:, col], nwm[:, col], nws[:, col] = adam_step(
            w[:, col], ref[:unit, :], wm[:, col], ws[:, col]
        )
    line = mine[unit : unit + 1, :unit] + theirs[unit : unit + 1, :unit]
    ng[...], ngm[...], ngs[...] = adam_step(g[...], line, gm[...], gs[...])


def paired_body(
    latents, noise, timesteps, master_weight, norm_gain, weight_moment, weight_second, gain_moment, gain_second
):
    rows, width = latents.shape
    unit = master_weight.shape[0]
    shards, cores = lax.axis_size("shard"), lax.axis_size("replica")
    total_rows = rows * shards * cores
    half = width // 2
    both = rows * cores
    me = lax.axis_index("shard")

    def to(x, k):
        pairs = [(i * cores + c, (i ^ k) * cores + c) for i in range(shards) for c in range(cores)]
        return lax.ppermute(x, AXES, pairs)

    def across(x):
        pairs = [(i * cores + c, i * cores + 1 - c) for i in range(shards) for c in range(cores)]
        return lax.ppermute(x, AXES, pairs)

    def call(kernel, outs, specs, scratch=(), flops=0, byts=0):
        return pl.pallas_call(
            kernel,
            out_shape=outs,
            in_specs=specs,
            out_specs=jax.tree.map(lambda _: VMEM, outs),
            scratch_shapes=list(scratch),
            compiler_params=pltpu.CompilerParams(vmem_limit_bytes=40 << 20),
            cost_estimate=pl.CostEstimate(flops=flops, bytes_accessed=byts, transcendentals=0),
        )

    arr = jax.ShapeDtypeStruct
    two, four = 2 * unit, 4 * unit

    own = call(
        pack_kernel,
        arr((unit + 16, half), BF),
        [HBM, HBM],
        [
            pltpu.VMEM((unit, half), F32),
            pltpu.VMEM((1, unit), F32),
            pltpu.SemaphoreType.DMA,
            pltpu.SemaphoreType.DMA,
        ],
        byts=6 * unit * half,
    )(
        pltpu.with_memory_space_constraint(master_weight, pltpu.HBM),
        pltpu.with_memory_space_constraint(norm_gain.reshape(1, unit), pltpu.HBM),
    )
    z1, z2, z3 = to(own, 4), to(own, 8), to(own, 12)
    wa, wb, tile = call(
        functools.partial(join_kernel, unit),
        (arr((two + 16, half), BF), arr((two + 16, half), BF), arr((16, half), BF)),
        [VMEM] * 4,
        byts=16 * unit * half,
    )(own, z1, z2, z3)
    wa1, wb1 = to(wa, 1), to(wb, 2)
    far = to(tile, 3)
    pair = call(pair_kernel, arr((four, half), BF), [VMEM] * 2 + [ANY], byts=16 * unit * half)
    pair_a, pair_b = pair(wa, wa1, tile), pair(wb, wb1, far)
    wa2, wb2 = to(pair_a, 2), to(pair_b, 1)

    other_latents, other_noise = across(latents), across(noise)
    step_time = lax.dynamic_slice(timesteps, (me * cores * rows // VOX,), (1,)).astype(F32)
    level = noise_level(step_time)
    coef = jnp.concatenate([jnp.sqrt(level), jnp.sqrt(1.0 - level)])
    angles = step_time[:, None] * frequencies(width)[None, :]
    embed = jnp.concatenate([jnp.sin(angles), jnp.cos(angles)], axis=1)
    act, slope, diff = call(
        functools.partial(act_kernel, unit),
        (arr((both, width), BF), arr((both, width), F32), arr((both, half), F32)),
        [SMEM] + [VMEM] * 9 + [ANY] * 2,
        [pltpu.VMEM((16, 128), F32), pltpu.VMEM((1, width), F32)],
        byts=28 * both * width,
    )(coef, embed, tile, wa1, wb1, far, latents, noise, other_latents, other_noise, pair_a, pair_b)

    send_a, send_b, keep_a, keep_b, mixing, gout = call(
        functools.partial(mix_kernel, 1.0 / math.sqrt(total_rows), unit),
        (
            arr((four, half), BF),
            arr((four, half), BF),
            arr((four, half), F32),
            arr((four, half), F32),
            arr((width, half), BF),
            arr((both, half), BF),
        ),
        [VMEM] * 8,
        [pltpu.VMEM((width, half), F32)],
        flops=4 * both * width * half,
        byts=6 * both * width,
    )(act, diff, wa, wa1, wa2, wb, wb1, wb2)

    got_a, got_b = to(send_a, 1), to(send_b, 2)
    pair_line = arr((2, 512), F32)
    thin_line = arr((1, 512), F32)
    keep_g, send_g = call(
        functools.partial(gain_kernel, unit),
        (pair_line, pair_line),
        [VMEM] * 3,
        [pltpu.VMEM((16, 128), F32)],
        flops=2 * both * width * half,
        byts=6 * both * width,
    )(gout, mixing, slope)
    got_g = to(send_g, 1)
    send_a, own_a, send_g, own_g = call(
        functools.partial(fold_a_kernel, unit),
        (arr((two, half), BF), arr((two, half), F32), thin_line, thin_line),
        [VMEM] * 4,
        byts=8 * four * half,
    )(keep_a, got_a, keep_g, got_g)
    got_a = to(send_a, 2)
    got_g = to(send_g, 2)
    send_b, own_b = call(
        functools.partial(fold_b_kernel, unit),
        (arr((two, half), BF), arr((two, half), F32)),
        [VMEM] * 2,
        byts=8 * four * half,
    )(keep_b, got_b)
    got_b = to(send_b, 1)
    send1, mine, line = call(
        functools.partial(turn_a_kernel, unit),
        (arr((unit + 16, half), BF), arr((unit, half), F32), arr((8, half), F32)),
        [VMEM] * 4,
        byts=8 * two * half,
    )(own_a, got_a, own_g, got_g)
    h1 = to(send1, 4)
    send2, send3 = call(
        functools.partial(turn_b_kernel, unit),
        (arr((unit + 16, half), BF), arr((unit + 16, half), BF)),
        [VMEM] * 3,
        byts=8 * two * half,
    )(own_b, got_b, line)
    h2, h3 = to(send2, 8), to(send3, 12)
    mine = call(
        functools.partial(last_kernel, unit),
        arr((unit + 8, half), F32),
        [VMEM] * 5,
        byts=16 * unit * half,
    )(mine, line, h1, h2, h3)
    theirs = across(mine)
    flat = arr((unit, width), F32)
    thin = arr((1, unit), F32)
    *weights, ng, ngm, ngs = call(
        functools.partial(adam_kernel, unit, half),
        (flat, flat, flat, thin, thin, thin),
        [VMEM] * 8,
        byts=24 * unit * width,
    )(
        mine, theirs, master_weight, weight_moment, weight_second,
        *(x.reshape(1, unit) for x in (norm_gain, gain_moment, gain_second)),
    )
    return (*weights, ng.reshape(unit), ngm.reshape(unit), ngs.reshape(unit))


def body(latents, *rest):
    rows, width = latents.shape
    unit = rest[2].shape[0]
    paired = (
        lax.axis_size("shard") == 16
        and lax.axis_size("replica") == 2
        and unit % 16 == 0
        and unit <= 128
        and width % 256 == 0
        and width >= 1024
        and rows % 16 == 0
        and VOX % (2 * rows) == 0
    )
    return (paired_body if paired else general_body)(latents, *rest)


def solution(mesh):
    rows = P(AXES, None)
    block = P("shard", None)
    line = P("shard")
    return jax.shard_map(
        body,
        mesh=mesh,
        in_specs=(rows, rows, P(), block, line, block, block, line, line),
        out_specs=(block, block, block, line, line, line),
        check_vma=False,
    )
```
